32 devices in a mesh: blk: 16 (over z, y, core), tok: 2 (over x).
Axes of the slice: x: 2, y: 2, z: 4, core: 2. Of those that a mesh axis runs over, the one named last changes fastest.
Arguments:
- tokens: bfloat16 [64, 8192], P(('blk', 'tok')), may hold values from -6 to 6
- upstream: bfloat16 [64, 8192], P(('blk', 'tok')), may hold values from -6 to 6
- gate_weight: bfloat16 [14336, 8192], P('blk'), may hold values from -0.0625 to 0.0625
- up_weight: bfloat16 [14336, 8192], P('blk'), may hold values from -0.0625 to 0.0625
- down_weight: bfloat16 [14336, 8192], P('blk'), may hold values from -0.046875 to 0.046875
Outputs:
- mixed: bfloat16 [64, 8192], P(('blk', 'tok'))
- input_grad: bfloat16 [64, 8192], P(('blk', 'tok'))
- gate_weight_grad: bfloat16 [14336, 8192], P('blk', 'tok')
- up_weight_grad: bfloat16 [14336, 8192], P('blk', 'tok')
- down_weight_grad: bfloat16 [14336, 8192], P('blk', 'tok')
The draws below stay inside these ranges and needn't reach their ends.
All inputs are finite; a program needn't handle non-finite values.
Results may differ from the reference program's by a relative error of at most 0.0049.
Values may be sent and summed in bfloat16 or wider, within the bound.
A program may use at most 192 MiB of HBM per device.

```python
import jax
import jax.numpy as jnp

D = 8192
FF = 14336
TOKENS = 64


def level_of(own_key, extent, shards, low, high):
    gain = 1.0
    for dim, shards_of in shards:
        draws = jax.random.uniform(jax.random.fold_in(jax.random.fold_in(own_key, 6), dim), (shards_of,), jnp.float32, low / len(shards), high / len(shards))
        gain = gain * jnp.repeat(jnp.exp(draws), extent[dim] // shards_of).reshape((-1,) + (1,) * (len(extent) - 1 - dim))
    return gain


def noise(own_key, shape, scale, most, pieces=(), kind=jnp.bfloat16):
    level = level_of(own_key, shape, pieces, -0.22, 0.18) if pieces else 1.0
    drawn = jax.random.normal(own_key, shape, jnp.float32) * scale * level
    return jnp.minimum(jnp.maximum(drawn, -most), most).astype(kind)


def setup_inputs(seed: int = 0) -> dict:
    streams_of = jax.random.split(jax.random.key(seed), 6)
    tokens = noise(streams_of[0], (TOKENS, D), 1.0, 6.0, ((0, 32),))
    upstream = noise(streams_of[1], (TOKENS, D), 1.0, 6.0, ((0, 32),))
    gate_weight = noise(streams_of[2], (FF, D), D ** -0.5, 0.0625, ((0, 16),))
    up_weight = noise(streams_of[3], (FF, D), D ** -0.5, 0.0625, ((0, 16),))
    down_weight = noise(streams_of[4], (FF, D), FF ** -0.5, 0.046875, ((0, 16),))
    return dict(tokens=tokens, upstream=upstream, gate_weight=gate_weight, up_weight=up_weight, down_weight=down_weight)


def reference(tokens, upstream, gate_weight, up_weight, down_weight):
    gate_value = jnp.dot(tokens, gate_weight.T, preferred_element_type=jnp.float32)
    up_value = jnp.dot(tokens, up_weight.T, preferred_element_type=jnp.float32)
    gate_sigmoid = jax.nn.sigmoid(gate_value)
    swish_gate = gate_value * gate_sigmoid
    hidden = (swish_gate * up_value).astype(jnp.bfloat16)
    mixed = jnp.dot(hidden, down_weight, preferred_element_type=jnp.float32).astype(jnp.bfloat16)
    hidden_grad = jnp.dot(upstream, down_weight.T, preferred_element_type=jnp.float32)
    gate_grad = (hidden_grad * up_value * gate_sigmoid * (1.0 + gate_value * (1.0 - gate_sigmoid))).astype(jnp.bfloat16)
    up_grad = (hidden_grad * swish_gate).astype(jnp.bfloat16)
    input_sum = jnp.dot(gate_grad, gate_weight, preferred_element_type=jnp.float32)
    input_sum = input_sum + jnp.dot(up_grad, up_weight, preferred_element_type=jnp.float32)
    input_grad = input_sum.astype(jnp.bfloat16)
    gate_weight_grad = jnp.dot(gate_grad.T, tokens, preferred_element_type=jnp.float32).astype(jnp.bfloat16)
    up_weight_grad = jnp.dot(up_grad.T, tokens, preferred_element_type=jnp.float32).astype(jnp.bfloat16)
    down_weight_grad = jnp.dot(hidden.T, upstream, preferred_element_type=jnp.float32).astype(jnp.bfloat16)
    return mixed, input_grad, gate_weight_grad, up_weight_grad, down_weight_grad
```

```python
import functools

import jax
import jax.numpy as jnp
from jax import lax
from jax.experimental import pallas as pl
from jax.experimental.pallas import tpu as pltpu
from jax.sharding import PartitionSpec as P

MESH = pl.DeviceIdType.MESH
VMEM_LIMIT = 63 * 1024 * 1024
GATHER_CHUNKS = 4
REDUCE_CHUNKS = 8
GRAD_CHUNKS = 4
GRAD_SLOTS = 3


def drain(ref, sem):
    pltpu.make_async_copy(ref, ref, sem).wait()


def columns(index, width):
    return pl.ds(pl.multiple_of(index * width, width), width)


def right_product(left, right):
    return lax.dot_general(
        left, right, (((1,), (1,)), ((), ())), preferred_element_type=jnp.float32
    )


def block_kernel(
    tokens,
    upstream,
    gate_hbm,
    up_hbm,
    down_hbm,
    mixed,
    input_grad,
    rows_out,
    hidden_out,
    weights,
    rows,
    values,
    hidden,
    own_term,
    pair_send,
    pair_recv,
    sum_send,
    sum_recv,
    weight_sem,
    send_sem,
    recv_sem,
    relay_send_sem,
    relay_recv_sem,
    half_sems,
    hidden_sems,
    pair_send_sem,
    pair_recv_sem,
    sum_send_sem,
    sum_recv_sem,
):
    count = lax.axis_size("blk")
    line = count // 2
    me = lax.axis_index("blk")
    tok = lax.axis_index("tok")
    place = me // 2
    core = me % 2
    sibling = (me + 1 - 2 * core, tok)
    across = (me, 1 - tok)
    own_rows, width = tokens.shape
    half_rows = line * own_rows
    group = 2 * half_rows
    half_width = width // 2
    gather_width = width // GATHER_CHUNKS
    reduce_width = width // REDUCE_CHUNKS
    inputs = (tokens, upstream)

    def peer(step):
        return ((place + step) % line * 2 + core, tok)

    def slot(index):
        return pl.ds(index * own_rows, own_rows)

    for part in range(GATHER_CHUNKS):
        cols = pl.ds(part * gather_width, gather_width)
        for index, hbm in enumerate((gate_hbm, up_hbm, down_hbm)):
            pltpu.make_async_copy(
                hbm.at[:, cols], weights.at[index, :, cols], weight_sem.at[index, part]
            ).start()
        for index, source in enumerate(inputs):
            pltpu.make_async_copy(
                source.at[:, cols], rows.at[index, slot(place), cols], recv_sem.at[index, part]
            ).start()

    barrier = pltpu.get_barrier_semaphore()

    def greet(step, carry):
        pl.semaphore_signal(barrier, inc=1, device_id=peer(step), device_id_type=MESH)
        return carry

    lax.fori_loop(1, line, greet, 0)
    pl.semaphore_signal(barrier, inc=1, device_id=sibling, device_id_type=MESH)
    pl.semaphore_signal(barrier, inc=1, device_id=across, device_id_type=MESH)
    pl.semaphore_wait(barrier, line + 1)

    for part in range(GATHER_CHUNKS):
        cols = pl.ds(part * gather_width, gather_width)

        def spread(step, carry):
            for index, source in enumerate(inputs):
                pltpu.make_async_remote_copy(
                    src_ref=source.at[:, cols],
                    dst_ref=rows.at[index, slot(place), cols],
                    send_sem=send_sem.at[index, step],
                    recv_sem=recv_sem.at[index, part],
                    device_id=peer(step),
                    device_id_type=MESH,
                ).start()
            return carry

        lax.fori_loop(1, line, spread, 0)

    def relay_copy(part, index):
        cols = pl.ds(part * gather_width, gather_width)
        return pltpu.make_async_remote_copy(
            src_ref=rows.at[index, pl.ds(0, half_rows), cols],
            dst_ref=rows.at[index, pl.ds(half_rows, half_rows), cols],
            send_sem=relay_send_sem.at[index, part],
            recv_sem=relay_recv_sem.at[index, part],
            device_id=sibling,
            device_id_type=MESH,
        )

    def relay(part):
        cols = pl.ds(part * gather_width, gather_width)
        for index in range(2):
            drain(rows.at[index, pl.ds(0, half_rows), cols], recv_sem.at[index, part])
            relay_copy(part, index).start()

    other_half = columns(1 - tok, half_width)
    own_half = columns(tok, half_width)
    half_local = [
        pltpu.make_async_copy(
            rows.at[index, :, own_half], rows_out.at[index, pl.ds(0, group)], half_sems.at[index, 0]
        )
        for index in range(2)
    ]
    half_remote = [
        pltpu.make_async_remote_copy(
            src_ref=rows.at[index, :, other_half],
            dst_ref=rows_out.at[index, pl.ds(group, group)],
            send_sem=half_sems.at[index, 1],
            recv_sem=half_sems.at[index, 2],
            device_id=across,
            device_id_type=MESH,
        )
        for index in range(2)
    ]

    relay(0)
    for part in range(GATHER_CHUNKS):
        cols = pl.ds(part * gather_width, gather_width)
        for index, hbm in enumerate((gate_hbm, up_hbm, down_hbm)):
            source = index // 2
            if index != 1:
                relay_copy(part, source).wait_recv()
            if part == GATHER_CHUNKS - 1 and index == 2:
                for copy in half_local + half_remote:
                    copy.start()
            pltpu.make_async_copy(
                hbm.at[:, cols], weights.at[index, :, cols], weight_sem.at[index, part]
            ).wait()
            term = right_product(rows[source, :, cols], weights[index, :, cols])
            if part == 0:
                values[index] = term
            else:
                values[index] += term
            if index == 0 and part + 1 < GATHER_CHUNKS:
                relay(part + 1)

    gate_value = values[0]
    up_value = values[1]
    hidden_grad = values[2]
    gate_sigmoid = jax.nn.sigmoid(gate_value)
    swish_gate = gate_value * gate_sigmoid
    hidden[0] = (
        hidden_grad * up_value * gate_sigmoid * (1.0 + gate_value * (1.0 - gate_sigmoid))
    ).astype(jnp.bfloat16)
    hidden[1] = (hidden_grad * swish_gate).astype(jnp.bfloat16)
    hidden[2] = (swish_gate * up_value).astype(jnp.bfloat16)
    hidden_local = [
        pltpu.make_async_copy(
            hidden.at[index], hidden_out.at[index, pl.ds(0, group)], hidden_sems.at[index, 0]
        )
        for index in range(3)
    ]
    hidden_remote = [
        pltpu.make_async_remote_copy(
            src_ref=hidden.at[index],
            dst_ref=hidden_out.at[index, pl.ds(group, group)],
            send_sem=hidden_sems.at[index, 1],
            recv_sem=hidden_sems.at[index, 2],
            device_id=across,
            device_id_type=MESH,
        )
        for index in range(3)
    ]
    for copy in hidden_local + hidden_remote:
        copy.start()

    def pair_copy(part, index):
        cols = columns(part, reduce_width)
        return pltpu.make_async_remote_copy(
            src_ref=pair_send.at[index, :, cols],
            dst_ref=pair_recv.at[index, :, cols],
            send_sem=pair_send_sem.at[index, part],
            recv_sem=pair_recv_sem.at[index, part],
            device_id=sibling,
            device_id_type=MESH,
        )

    def produce(part):
        cols = columns(part, reduce_width)
        term = jnp.dot(hidden[2], weights[2, :, cols], preferred_element_type=jnp.float32)
        own_term[0, :, cols] = term[:half_rows]
        pair_send[0, :, cols] = term[half_rows:].astype(jnp.bfloat16)
        pair_copy(part, 0).start()
        term = jnp.dot(hidden[0], weights[0, :, cols], preferred_element_type=jnp.float32)
        term += jnp.dot(hidden[1], weights[1, :, cols], preferred_element_type=jnp.float32)
        own_term[1, :, cols] = term[:half_rows]
        pair_send[1, :, cols] = term[half_rows:].astype(jnp.bfloat16)
        pair_copy(part, 1).start()

    def deliver(part):
        cols = columns(part, reduce_width)
        for index in range(2):
            pair_copy(part, index).wait_recv()
            sum_send[index, :, cols] = (
                own_term[index, :, cols] + pair_recv[index, :, cols].astype(jnp.float32)
            ).astype(jnp.bfloat16)
            pltpu.make_async_copy(
                sum_send.at[index, slot(place), cols],
                sum_recv.at[index, slot(place), cols],
                sum_recv_sem.at[index],
            ).start()

            def hand(step, carry):
                pltpu.make_async_remote_copy(
                    src_ref=sum_send.at[index, slot((place + step) % line), cols],
                    dst_ref=sum_recv.at[index, slot(place), cols],
                    send_sem=sum_send_sem.at[index, step],
                    recv_sem=sum_recv_sem.at[index],
                    device_id=peer(step),
                    device_id_type=MESH,
                ).start()
                return carry

            lax.fori_loop(1, line, hand, 0)

    produce(0)

    def advance(part, carry):
        produce(part)
        deliver(part - 1)
        return carry

    lax.fori_loop(1, REDUCE_CHUNKS, advance, 0)
    deliver(REDUCE_CHUNKS - 1)

    for index in range(2):
        drain(sum_recv.at[index], sum_recv_sem.at[index])
    pick = (
        lax.broadcasted_iota(jnp.int32, (own_rows, half_rows), 1) % own_rows
        == lax.broadcasted_iota(jnp.int32, (own_rows, half_rows), 0)
    ).astype(jnp.bfloat16)
    for index, result in enumerate((mixed, input_grad)):
        result[...] = jnp.dot(pick, sum_recv[index], preferred_element_type=jnp.float32).astype(
            jnp.bfloat16
        )

    for index in range(2):

        def sent(step, carry):
            drain(inputs[index], send_sem.at[index, step])
            drain(inputs[index], sum_send_sem.at[index, step])
            return carry

        lax.fori_loop(1, line, sent, 0)
        for part in range(GATHER_CHUNKS):
            relay_copy(part, index).wait_send()
        for part in range(REDUCE_CHUNKS):
            pair_copy(part, index).wait_send()
    for copy in half_local + half_remote + hidden_local + hidden_remote:
        copy.wait()


def block(tokens, upstream, gate_weight, up_weight, down_weight):
    own_rows, width = tokens.shape
    units = gate_weight.shape[0]
    count = lax.axis_size("blk")
    assert count % 2 == 0 and lax.axis_size("tok") == 2
    half_rows = count // 2 * own_rows
    group = 2 * half_rows
    bf16, f32 = jnp.bfloat16, jnp.float32
    hbm = pl.BlockSpec(memory_space=pl.ANY)
    vmem = pl.BlockSpec(memory_space=pltpu.VMEM)
    dma = pltpu.SemaphoreType.DMA
    return pl.pallas_call(
        block_kernel,
        out_shape=(
            jax.ShapeDtypeStruct((own_rows, width), bf16),
            jax.ShapeDtypeStruct((own_rows, width), bf16),
            jax.ShapeDtypeStruct((2, 2 * group, width // 2), bf16),
            jax.ShapeDtypeStruct((3, 2 * group, units), bf16),
        ),
        in_specs=[hbm] * 5,
        out_specs=(vmem, vmem, hbm, hbm),
        scratch_shapes=[
            pltpu.VMEM((3, units, width), bf16),
            pltpu.VMEM((2, group, width), bf16),
            pltpu.VMEM((3, group, units), f32),
            pltpu.VMEM((3, group, units), bf16),
            pltpu.VMEM((2, half_rows, width), f32),
            pltpu.VMEM((2, half_rows, width), bf16),
            pltpu.VMEM((2, half_rows, width), bf16),
            pltpu.VMEM((2, half_rows, width), bf16),
            pltpu.VMEM((2, half_rows, width), bf16),
            dma((3, GATHER_CHUNKS)),
            dma((2, count // 2)),
            dma((2, GATHER_CHUNKS)),
            dma((2, GATHER_CHUNKS)),
            dma((2, GATHER_CHUNKS)),
            dma((2, 3)),
            dma((3, 3)),
            dma((2, REDUCE_CHUNKS)),
            dma((2, REDUCE_CHUNKS)),
            dma((2, count // 2)),
            dma((2,)),
        ],
        compiler_params=pltpu.CompilerParams(
            collective_id=0, has_side_effects=True, vmem_limit_bytes=VMEM_LIMIT
        ),
    )(tokens, upstream, gate_weight, up_weight, down_weight)


def grad_kernel(rows, hidden, gate_grad, up_grad, down_grad, tiles, sems):
    width = rows.shape[2] // GRAD_CHUNKS
    pending = [None] * GRAD_SLOTS
    step = 0
    for index, result in enumerate((gate_grad, up_grad, down_grad)):
        for part in range(GRAD_CHUNKS):
            cols = pl.ds(part * width, width)
            where = step % GRAD_SLOTS
            if pending[where] is not None:
                pending[where].wait()
            tiles[where] = lax.dot_general(
                hidden[index],
                rows[index // 2, :, cols],
                (((0,), (0,)), ((), ())),
                preferred_element_type=jnp.float32,
            ).astype(jnp.bfloat16)
            pending[where] = pltpu.make_async_copy(
                tiles.at[where], result.at[:, cols], sems.at[where]
            )
            pending[where].start()
            step += 1
    for copy in pending:
        if copy is not None:
            copy.wait()


def weight_grads(rows, hidden):
    units = hidden.shape[2]
    width = rows.shape[2]
    hbm = pl.BlockSpec(memory_space=pl.ANY)
    vmem = pl.BlockSpec(memory_space=pltpu.VMEM)
    shape = jax.ShapeDtypeStruct((units, width), jnp.bfloat16)
    return pl.pallas_call(
        grad_kernel,
        out_shape=(shape, shape, shape),
        in_specs=[vmem, vmem],
        out_specs=(hbm, hbm, hbm),
        scratch_shapes=[
            pltpu.VMEM((GRAD_SLOTS, units, width // GRAD_CHUNKS), jnp.bfloat16),
            pltpu.SemaphoreType.DMA((GRAD_SLOTS,)),
        ],
        compiler_params=pltpu.CompilerParams(vmem_limit_bytes=VMEM_LIMIT),
    )(rows, hidden)


def local(*args):
    mixed, input_grad, rows, hidden = block(*args)
    return (mixed, input_grad, *weight_grads(rows, hidden))


def solution(mesh):
    return jax.shard_map(
        local,
        mesh=mesh,
        in_specs=(
            P(("blk", "tok"), None),
            P(("blk", "tok"), None),
            P("blk", None),
            P("blk", None),
            P("blk", None),
        ),
        out_specs=(
            P(("blk", "tok"), None),
            P(("blk", "tok"), None),
            P("blk", "tok"),
            P("blk", "tok"),
            P("blk", "tok"),
        ),
        check_vma=False,
    )
```

```python
import functools

import jax
import jax.numpy as jnp
from jax import lax
from jax.experimental import pallas as pl
from jax.experimental.pallas import tpu as pltpu
from jax.sharding import PartitionSpec as P

MESH = pl.DeviceIdType.MESH
VMEM_LIMIT = 63 * 1024 * 1024
GATHER_PARTS = (1, 1, 2, 2, 2)
REDUCE_PARTS = (2, 2, 2, 1, 1)
FOLD_PAIR_LAG = 1
FOLD_SIDE_LAG = 3
GRAD_CHUNKS = 4
GRAD_SLOTS = 3


def drain(ref, sem):
    pltpu.make_async_copy(ref, ref, sem).wait()


def columns(index, width):
    return pl.ds(pl.multiple_of(index * width, width), width)


def pieces(width, shares):
    unit = width // sum(shares)
    starts = [sum(shares[:index]) for index in range(len(shares))]
    return [pl.ds(start * unit, share * unit) for start, share in zip(starts, shares)]


def right_product(left, right):
    return lax.dot_general(
        left, right, (((1,), (1,)), ((), ())), preferred_element_type=jnp.float32
    )


def block_kernel(
    tokens,
    upstream,
    gate_hbm,
    up_hbm,
    down_hbm,
    rows_out,
    hidden_out,
    sums_out,
    weights,
    rows,
    values,
    hidden,
    far_rows,
    own_term,
    pair_send,
    pair_recv,
    side_send,
    side_recv,
    line_send,
    weight_sem,
    send_sem,
    recv_sem,
    side_sems,
    pair_sems,
    far_sems,
    hidden_sems,
    term_pair_sems,
    term_side_sems,
    sum_send_sem,
    sum_recv_sem,
):
    line = lax.axis_size("blk") // 4
    me = lax.axis_index("blk")
    tok = lax.axis_index("tok")
    core = me % 2
    side = me // 2 % 2
    place = me // 4
    sibling = (me + 1 - 2 * core, tok)
    beside = (me + 2 - 4 * side, tok)
    across = (me, 1 - tok)
    own_rows, width = tokens.shape
    quarter = line * own_rows
    half = 2 * quarter
    group = 2 * half
    half_width = width // 2
    inputs = (tokens, upstream)
    gather_cols = pieces(width, GATHER_PARTS)
    reduce_cols = pieces(width, REDUCE_PARTS)
    sources = (gate_hbm, up_hbm, down_hbm)

    def peer(step):
        return ((place + step) % line * 4 + side * 2 + core, tok)

    def slot(index):
        return pl.ds(index * own_rows, own_rows)

    def remote(source, target, sems, where, device):
        return pltpu.make_async_remote_copy(
            src_ref=source,
            dst_ref=target,
            send_sem=sems.at[(0, *where)],
            recv_sem=sems.at[(1, *where)],
            device_id=device,
            device_id_type=MESH,
        )

    def weight_copy(index, part):
        cols = gather_cols[part]
        return pltpu.make_async_copy(
            sources[index].at[:, cols], weights.at[index, :, cols], weight_sem.at[index, part]
        )

    parts = range(len(gather_cols))
    for part in parts:
        for index, source in enumerate(inputs):
            cols = gather_cols[part]
            pltpu.make_async_copy(
                source.at[:, cols], rows.at[index, slot(place), cols], recv_sem.at[index, part]
            ).start()
    for part in parts:
        for index in range(3):
            weight_copy(index, part).start()

    barrier = pltpu.get_barrier_semaphore()

    def greet(step, carry):
        pl.semaphore_signal(barrier, inc=1, device_id=peer(step), device_id_type=MESH)
        return carry

    lax.fori_loop(1, line, greet, 0)
    for device in (beside, sibling, across):
        pl.semaphore_signal(barrier, inc=1, device_id=device, device_id_type=MESH)
    pl.semaphore_wait(barrier, line + 2)

    for part in parts:
        cols = gather_cols[part]

        def spread(step, carry):
            for index, source in enumerate(inputs):
                pltpu.make_async_remote_copy(
                    src_ref=source.at[:, cols],
                    dst_ref=rows.at[index, slot(place), cols],
                    send_sem=send_sem.at[index, step],
                    recv_sem=recv_sem.at[index, part],
                    device_id=peer(step),
                    device_id_type=MESH,
                ).start()
            return carry

        lax.fori_loop(1, line, spread, 0)

    def side_copy(index, part):
        cols = gather_cols[part]
        return remote(
            rows.at[index, pl.ds(0, quarter), cols],
            rows.at[index, pl.ds(quarter, quarter), cols],
            side_sems,
            (index, part),
            beside,
        )

    def pair_copy(index, part):
        cols = gather_cols[part]
        return remote(
            rows.at[index, pl.ds(0, half), cols],
            rows.at[index, pl.ds(half, half), cols],
            pair_sems,
            (index, part),
            sibling,
        )

    def to_side(part):
        if part < len(gather_cols):
            for index in range(2):
                drain(rows.at[index, pl.ds(0, quarter), gather_cols[part]], recv_sem.at[index, part])
                side_copy(index, part).start()

    def to_pair(part):
        if part < len(gather_cols):
            for index in range(2):
                side_copy(index, part).wait_recv()
                pair_copy(index, part).start()

    other_half = columns(1 - tok, half_width)
    own_half = columns(tok, half_width)
    far_copy = [
        remote(
            rows.at[index, pl.ds(0, half), other_half], far_rows.at[index], far_sems, (index,), across
        )
        for index in range(2)
    ]
    far_keep = [
        pltpu.make_async_copy(
            far_rows.at[index], rows_out.at[index, pl.ds(group, half)], far_sems.at[2, index]
        )
        for index in range(2)
    ]
    far_relay = [
        pltpu.make_async_remote_copy(
            src_ref=far_rows.at[index],
            dst_ref=rows_out.at[index, pl.ds(group + half, half)],
            send_sem=far_sems.at[3, index],
            recv_sem=far_sems.at[4, index],
            device_id=sibling,
            device_id_type=MESH,
        )
        for index in range(2)
    ]
    near_keep = [
        pltpu.make_async_copy(
            rows.at[index, :, own_half], rows_out.at[index, pl.ds(0, group)], far_sems.at[5, index]
        )
        for index in range(2)
    ]

    to_side(0)
    to_side(1)
    to_pair(0)
    to_side(2)
    to_pair(1)
    for part in parts:
        cols = gather_cols[part]
        last = part == len(gather_cols) - 1
        for index in range(3):
            source = index // 2
            if index != 1:
                pair_copy(source, part).wait_recv()
            if last and index == 0:
                for copy in far_copy:
                    copy.start()
            if last and index == 2:
                for copy in near_keep:
                    copy.start()
            weight_copy(index, part).wait()
            term = right_product(rows[source, :, cols], weights[index, :, cols])
            if part == 0:
                values[index] = term
            else:
                values[index] += term
            if index == 0:
                to_side(part + 3)
            if index == 1:
                to_pair(part + 2)

    gate_value = values[0]
    up_value = values[1]
    hidden_grad = values[2]
    gate_sigmoid = jax.nn.sigmoid(gate_value)
    swish_gate = gate_value * gate_sigmoid
    hidden[0] = (
        hidden_grad * up_value * gate_sigmoid * (1.0 + gate_value * (1.0 - gate_sigmoid))
    ).astype(jnp.bfloat16)
    hidden[1] = (hidden_grad * swish_gate).astype(jnp.bfloat16)
    hidden[2] = (swish_gate * up_value).astype(jnp.bfloat16)
    hidden_local = [
        pltpu.make_async_copy(
            hidden.at[index], hidden_out.at[index, pl.ds(0, group)], hidden_sems.at[2, index]
        )
        for index in range(3)
    ]
    hidden_remote = [
        remote(
            hidden.at[index],
            hidden_out.at[index, pl.ds(group, group)],
            hidden_sems,
            (index,),
            across,
        )
        for index in range(3)
    ]
    for copy in hidden_local + hidden_remote:
        copy.start()

    def term_pair(index, part):
        cols = reduce_cols[part]
        return remote(
            pair_send.at[index, :, cols],
            pair_recv.at[index, :, cols],
            term_pair_sems,
            (index, part),
            sibling,
        )

    def term_side(index, part):
        cols = reduce_cols[part]
        return remote(
            side_send.at[index, :, cols],
            side_recv.at[index, :, cols],
            term_side_sems,
            (index, part),
            beside,
        )

    def product(index, cols):
        return jnp.dot(hidden[index], weights[index, :, cols], preferred_element_type=jnp.float32)

    def produce(index, part):
        cols = reduce_cols[part]
        if index == 0:
            term = product(2, cols)
        else:
            term = product(0, cols) + product(1, cols)
        own_term[index, :, cols] = term[:half]
        pair_send[index, :, cols] = term[half:].astype(jnp.bfloat16)
        term_pair(index, part).start()

    def fold_pair(index, part):
        cols = reduce_cols[part]
        term_pair(index, part).wait_recv()
        term = own_term[index, :, cols] + pair_recv[index, :, cols].astype(jnp.float32)
        own_term[index, :quarter, cols] = term[:quarter]
        side_send[index, :, cols] = term[quarter:].astype(jnp.bfloat16)
        term_side(index, part).start()

    def fold_side(index, part):
        cols = reduce_cols[part]
        term_side(index, part).wait_recv()
        line_send[index, :, cols] = (
            own_term[index, :quarter, cols] + side_recv[index, :, cols].astype(jnp.float32)
        ).astype(jnp.bfloat16)
        pltpu.make_async_copy(
            line_send.at[index, slot(place), cols],
            sums_out.at[index, slot(place), cols],
            sum_recv_sem.at[index],
        ).start()

        def hand(step, carry):
            pltpu.make_async_remote_copy(
                src_ref=line_send.at[index, slot((place + step) % line), cols],
                dst_ref=sums_out.at[index, slot(place), cols],
                send_sem=sum_send_sem.at[index, step],
                recv_sem=sum_recv_sem.at[index],
                device_id=peer(step),
                device_id_type=MESH,
            ).start()
            return carry

        lax.fori_loop(1, line, hand, 0)

    units = [(index, part) for part in range(len(reduce_cols)) for index in (1, 0)]
    for step in range(len(units) + FOLD_SIDE_LAG):
        if step < len(units):
            produce(*units[step])
        if step == 0:
            for index in range(2):
                far_copy[index].wait_recv()
                far_keep[index].start()
                far_relay[index].start()
        if 0 <= step - FOLD_PAIR_LAG < len(units):
            fold_pair(*units[step - FOLD_PAIR_LAG])
        if 0 <= step - FOLD_SIDE_LAG < len(units):
            fold_side(*units[step - FOLD_SIDE_LAG])

    for index in range(2):

        def sent(step, carry):
            drain(inputs[index], send_sem.at[index, step])
            drain(inputs[index], sum_send_sem.at[index, step])
            return carry

        lax.fori_loop(1, line, sent, 0)
        for part in parts:
            side_copy(index, part).wait_send()
            pair_copy(index, part).wait_send()
        for part in range(len(reduce_cols)):
            term_pair(index, part).wait_send()
            term_side(index, part).wait_send()
        far_copy[index].wait_send()
    for copy in far_keep + far_relay + near_keep + hidden_local + hidden_remote:
        copy.wait()
    for index in range(2):
        drain(sums_out.at[index], sum_recv_sem.at[index])


def block(tokens, upstream, gate_weight, up_weight, down_weight):
    own_rows, width = tokens.shape
    units = gate_weight.shape[0]
    count = lax.axis_size("blk")
    assert count % 4 == 0 and lax.axis_size("tok") == 2
    line = count // 4
    quarter = line * own_rows
    half = 2 * quarter
    group = 2 * half
    gathers, reduces = len(GATHER_PARTS), len(REDUCE_PARTS)
    bf16, f32 = jnp.bfloat16, jnp.float32
    hbm = pl.BlockSpec(memory_space=pl.ANY)
    dma = pltpu.SemaphoreType.DMA
    return pl.pallas_call(
        block_kernel,
        out_shape=(
            jax.ShapeDtypeStruct((2, 2 * group, width // 2), bf16),
            jax.ShapeDtypeStruct((3, 2 * group, units), bf16),
            jax.ShapeDtypeStruct((2, quarter, width), bf16),
        ),
        in_specs=[hbm] * 5,
        out_specs=(hbm, hbm, hbm),
        scratch_shapes=[
            pltpu.VMEM((3, units, width), bf16),
            pltpu.VMEM((2, group, width), bf16),
            pltpu.VMEM((3, group, units), f32),
            pltpu.VMEM((3, group, units), bf16),
            pltpu.VMEM((2, half, width // 2), bf16),
            pltpu.VMEM((2, half, width), f32),
            pltpu.VMEM((2, half, width), bf16),
            pltpu.VMEM((2, half, width), bf16),
            pltpu.VMEM((2, quarter, width), bf16),
            pltpu.VMEM((2, quarter, width), bf16),
            pltpu.VMEM((2, quarter, width), bf16),
            dma((3, gathers)),
            dma((2, line)),
            dma((2, gathers)),
            dma((2, 2, gathers)),
            dma((2, 2, gathers)),
            dma((6, 2)),
            dma((3, 3)),
            dma((2, 2, reduces)),
            dma((2, 2, reduces)),
            dma((2, line)),
            dma((2,)),
        ],
        compiler_params=pltpu.CompilerParams(
            collective_id=0, has_side_effects=True, vmem_limit_bytes=VMEM_LIMIT
        ),
    )(tokens, upstream, gate_weight, up_weight, down_weight)


def grad_kernel(
    rows_hbm,
    hidden_hbm,
    sums_hbm,
    mixed,
    input_grad,
    gate_grad,
    up_grad,
    down_grad,
    rows,
    hidden,
    sums,
    tiles,
    load_sems,
    sems,
):
    loads = [
        pltpu.make_async_copy(rows_hbm.at[0], rows.at[0], load_sems.at[0]),
        pltpu.make_async_copy(hidden_hbm.at[0], hidden.at[0], load_sems.at[1]),
        pltpu.make_async_copy(hidden_hbm.at[1], hidden.at[1], load_sems.at[2]),
        pltpu.make_async_copy(rows_hbm.at[1], rows.at[1], load_sems.at[3]),
        pltpu.make_async_copy(hidden_hbm.at[2], hidden.at[2], load_sems.at[4]),
        pltpu.make_async_copy(sums_hbm, sums, load_sems.at[5]),
    ]
    for copy in loads:
        copy.start()
    width = rows.shape[2] // GRAD_CHUNKS
    pending = [None] * GRAD_SLOTS
    step = 0
    for index, result in enumerate((gate_grad, up_grad, down_grad)):
        for copy in (loads[:2], loads[2:3], loads[3:5])[index]:
            copy.wait()
        for part in range(GRAD_CHUNKS):
            cols = pl.ds(part * width, width)
            where = step % GRAD_SLOTS
            if pending[where] is not None:
                pending[where].wait()
            tiles[where] = lax.dot_general(
                hidden[index],
                rows[index // 2, :, cols],
                (((0,), (0,)), ((), ())),
                preferred_element_type=jnp.float32,
            ).astype(jnp.bfloat16)
            pending[where] = pltpu.make_async_copy(
                tiles.at[where], result.at[:, cols], sems.at[where]
            )
            pending[where].start()
            step += 1
    own_rows, quarter = mixed.shape[0], sums.shape[1]
    pick = (
        lax.broadcasted_iota(jnp.int32, (own_rows, quarter), 1) % own_rows
        == lax.broadcasted_iota(jnp.int32, (own_rows, quarter), 0)
    ).astype(jnp.bfloat16)
    loads[5].wait()
    for index, result in enumerate((mixed, input_grad)):
        result[...] = jnp.dot(pick, sums[index], preferred_element_type=jnp.float32).astype(
            jnp.bfloat16
        )
    for copy in pending:
        if copy is not None:
            copy.wait()


def finish(rows, hidden, sums, own_rows):
    units = hidden.shape[2]
    width = rows.shape[2]
    hbm = pl.BlockSpec(memory_space=pl.ANY)
    vmem = pl.BlockSpec(memory_space=pltpu.VMEM)
    small = jax.ShapeDtypeStruct((own_rows, sums.shape[2]), jnp.bfloat16)
    shape = jax.ShapeDtypeStruct((units, width), jnp.bfloat16)
    return pl.pallas_call(
        grad_kernel,
        out_shape=(small, small, shape, shape, shape),
        in_specs=[hbm, hbm, hbm],
        out_specs=(vmem, vmem, hbm, hbm, hbm),
        scratch_shapes=[
            pltpu.VMEM(rows.shape, jnp.bfloat16),
            pltpu.VMEM(hidden.shape, jnp.bfloat16),
            pltpu.VMEM(sums.shape, jnp.bfloat16),
            pltpu.VMEM((GRAD_SLOTS, units, width // GRAD_CHUNKS), jnp.bfloat16),
            pltpu.SemaphoreType.DMA((6,)),
            pltpu.SemaphoreType.DMA((GRAD_SLOTS,)),
        ],
        compiler_params=pltpu.CompilerParams(vmem_limit_bytes=VMEM_LIMIT),
    )(rows, hidden, sums)


def local(tokens, *rest):
    rows, hidden, sums = block(tokens, *rest)
    return finish(rows, hidden, sums, tokens.shape[0])


def solution(mesh):
    return jax.shard_map(
        local,
        mesh=mesh,
        in_specs=(
            P(("blk", "tok"), None),
            P(("blk", "tok"), None),
            P("blk", None),
            P("blk", None),
            P("blk", None),
        ),
        out_specs=(
            P(("blk", "tok"), None),
            P(("blk", "tok"), None),
            P("blk", "tok"),
            P("blk", "tok"),
            P("blk", "tok"),
        ),
        check_vma=False,
    )
```

```python
import functools

import jax
import jax.numpy as jnp
from jax import lax
from jax.experimental import pallas as pl
from jax.experimental.pallas import tpu as pltpu
from jax.sharding import PartitionSpec as P

MESH = pl.DeviceIdType.MESH
VMEM_LIMIT = 63 * 1024 * 1024
GATHER_PARTS = (2, 3, 3)
REDUCE_PARTS = (4, 2, 2)
FOLD_PAIR_LAG = 1
FOLD_SIDE_LAG = 2
UNROLLED_LINE = 8
GRAD_CHUNKS = 4
GRAD_SLOTS = 3


def drain(ref, sem):
    pltpu.make_async_copy(ref, ref, sem).wait()


def columns(index, width):
    return pl.ds(pl.multiple_of(index * width, width), width)


def pieces(width, shares):
    unit = width // sum(shares)
    starts = [sum(shares[:index]) for index in range(len(shares))]
    return [pl.ds(start * unit, share * unit) for start, share in zip(starts, shares)]


def right_product(left, right):
    return lax.dot_general(
        left, right, (((1,), (1,)), ((), ())), preferred_element_type=jnp.float32
    )


def block_kernel(
    tokens,
    upstream,
    gate_hbm,
    up_hbm,
    down_hbm,
    rows_out,
    hidden_out,
    sums_out,
    weights,
    rows,
    values,
    hidden,
    far_rows,
    own_term,
    pair_send,
    pair_recv,
    side_send,
    side_recv,
    line_send,
    weight_sem,
    own_sem,
    send_sem,
    recv_sem,
    side_sems,
    pair_sems,
    far_sems,
    hidden_sems,
    term_pair_sems,
    term_side_sems,
    sum_send_sem,
    sum_recv_sem,
):
    line = lax.axis_size("blk") // 4
    me = lax.axis_index("blk")
    tok = lax.axis_index("tok")
    core = me % 2
    side = me // 2 % 2
    place = me // 4
    sibling = (me + 1 - 2 * core, tok)
    beside = (me + 2 - 4 * side, tok)
    across = (me, 1 - tok)
    own_rows, width = tokens.shape
    quarter = line * own_rows
    half = 2 * quarter
    group = 2 * half
    half_width = width // 2
    gather_cols = pieces(width, GATHER_PARTS)
    reduce_cols = pieces(width, REDUCE_PARTS)
    parts = range(len(gather_cols))
    sources = (gate_hbm, up_hbm, down_hbm)

    def peer(step):
        return ((place + step) % line * 4 + side * 2 + core, tok)

    def slot(index):
        return pl.ds(index * own_rows, own_rows)

    def each_step(body):
        if line <= UNROLLED_LINE:
            for step in range(1, line):
                body(step)
        else:

            def turn(step, carry):
                body(step)
                return carry

            lax.fori_loop(1, line, turn, 0)

    def remote(source, target, sems, where, device):
        return pltpu.make_async_remote_copy(
            src_ref=source,
            dst_ref=target,
            send_sem=sems.at[(0, *where)],
            recv_sem=sems.at[(1, *where)],
            device_id=device,
            device_id_type=MESH,
        )

    def weight_copy(index, part):
        cols = gather_cols[part]
        return pltpu.make_async_copy(
            sources[index].at[:, cols], weights.at[index, :, cols], weight_sem.at[index, part]
        )

    own_copies = [
        pltpu.make_async_copy(source, rows.at[index, slot(place)], own_sem.at[index])
        for index, source in enumerate((tokens, upstream))
    ]
    for copy in own_copies:
        copy.start()
    barrier = pltpu.get_barrier_semaphore()

    def greet(step):
        pl.semaphore_signal(barrier, inc=1, device_id=peer(step), device_id_type=MESH)

    each_step(greet)
    for device in (beside, sibling, across):
        pl.semaphore_signal(barrier, inc=1, device_id=device, device_id_type=MESH)
    for part in parts:
        for index in range(3):
            weight_copy(index, part).start()
    for copy in own_copies:
        copy.wait()
    pl.semaphore_wait(barrier, line + 2)

    for part in parts:
        cols = gather_cols[part]

        def spread(step):
            pltpu.make_async_remote_copy(
                src_ref=rows.at[:, slot(place), cols],
                dst_ref=rows.at[:, slot(place), cols],
                send_sem=send_sem.at[step],
                recv_sem=recv_sem.at[part, step],
                device_id=peer(step),
                device_id_type=MESH,
            ).start()

        each_step(spread)

    def side_copy(part):
        cols = gather_cols[part]
        return remote(
            rows.at[:, pl.ds(0, quarter), cols],
            rows.at[:, pl.ds(quarter, quarter), cols],
            side_sems,
            (part,),
            beside,
        )

    def pair_copy(part):
        cols = gather_cols[part]
        return remote(
            rows.at[:, pl.ds(0, half), cols],
            rows.at[:, pl.ds(half, half), cols],
            pair_sems,
            (part,),
            sibling,
        )

    def to_side(part):
        if part < len(gather_cols):
            cols = gather_cols[part]
            each_step(lambda step: drain(rows.at[:, slot(place), cols], recv_sem.at[part, step]))
            side_copy(part).start()

    def to_pair(part):
        if part < len(gather_cols):
            side_copy(part).wait_recv()
            pair_copy(part).start()

    other_half = columns(1 - tok, half_width)
    own_half = columns(tok, half_width)
    far_copy = remote(rows.at[:, pl.ds(0, half), other_half], far_rows, far_sems, (), across)
    far_keep = pltpu.make_async_copy(far_rows, rows_out.at[:, pl.ds(group, half)], far_sems.at[2])
    far_relay = pltpu.make_async_remote_copy(
        src_ref=far_rows,
        dst_ref=rows_out.at[:, pl.ds(group + half, half)],
        send_sem=far_sems.at[3],
        recv_sem=far_sems.at[4],
        device_id=sibling,
        device_id_type=MESH,
    )
    near_keep = pltpu.make_async_copy(
        rows.at[:, :, own_half], rows_out.at[:, pl.ds(0, group)], far_sems.at[5]
    )

    to_side(0)
    to_side(1)
    to_pair(0)
    for part in parts:
        cols = gather_cols[part]
        last = part == len(gather_cols) - 1
        pair_copy(part).wait_recv()
        if last:
            far_copy.start()
            near_keep.start()
        for index in range(3):
            weight_copy(index, part).wait()
            term = right_product(rows[index // 2, :, cols], weights[index, :, cols])
            if part == 0:
                values[index] = term
            else:
                values[index] += term
            if index == 0:
                to_pair(part + 1)
            if index == 1:
                to_side(part + 2)

    gate_value = values[0]
    up_value = values[1]
    hidden_grad = values[2]
    gate_sigmoid = jax.nn.sigmoid(gate_value)
    swish_gate = gate_value * gate_sigmoid
    hidden[0] = (
        hidden_grad * up_value * gate_sigmoid * (1.0 + gate_value * (1.0 - gate_sigmoid))
    ).astype(jnp.bfloat16)
    hidden[1] = (hidden_grad * swish_gate).astype(jnp.bfloat16)
    hidden[2] = (swish_gate * up_value).astype(jnp.bfloat16)
    hidden_local = pltpu.make_async_copy(
        hidden, hidden_out.at[:, pl.ds(0, group)], hidden_sems.at[2]
    )
    hidden_remote = remote(
        hidden, hidden_out.at[:, pl.ds(group, group)], hidden_sems, (), across
    )
    hidden_local.start()
    hidden_remote.start()

    def term_pair(part):
        cols = reduce_cols[part]
        return remote(
            pair_send.at[:, :, cols], pair_recv.at[:, :, cols], term_pair_sems, (part,), sibling
        )

    def term_side(part):
        cols = reduce_cols[part]
        return remote(
            side_send.at[:, :, cols], side_recv.at[:, :, cols], term_side_sems, (part,), beside
        )

    def product(index, cols):
        return jnp.dot(hidden[index], weights[index, :, cols], preferred_element_type=jnp.float32)

    def produce(part):
        cols = reduce_cols[part]
        for index in range(2):
            if index == 0:
                term = product(2, cols)
            else:
                term = product(0, cols) + product(1, cols)
            own_term[index, :, cols] = term[:half]
            pair_send[index, :, cols] = term[half:].astype(jnp.bfloat16)
        term_pair(part).start()

    def fold_pair(part):
        cols = reduce_cols[part]
        term_pair(part).wait_recv()
        for index in range(2):
            term = own_term[index, :, cols] + pair_recv[index, :, cols].astype(jnp.float32)
            own_term[index, :quarter, cols] = term[:quarter]
            side_send[index, :, cols] = term[quarter:].astype(jnp.bfloat16)
        term_side(part).start()

    def fold_side(part):
        cols = reduce_cols[part]
        term_side(part).wait_recv()
        for index in range(2):
            line_send[index, :, cols] = (
                own_term[index, :quarter, cols] + side_recv[index, :, cols].astype(jnp.float32)
            ).astype(jnp.bfloat16)

        def hand(step):
            pltpu.make_async_remote_copy(
                src_ref=line_send.at[:, slot((place + step) % line), cols],
                dst_ref=sums_out.at[:, slot(place), cols],
                send_sem=sum_send_sem.at[step],
                recv_sem=sum_recv_sem,
                device_id=peer(step),
                device_id_type=MESH,
            ).start()

        each_step(hand)
        pltpu.make_async_copy(
            line_send.at[:, slot(place), cols], sums_out.at[:, slot(place), cols], sum_recv_sem
        ).start()

    units = len(reduce_cols)
    for step in range(units + FOLD_SIDE_LAG):
        if step < units:
            produce(step)
        if step == 0:
            far_copy.wait_recv()
            far_keep.start()
            far_relay.start()
        if 0 <= step - FOLD_PAIR_LAG < units:
            fold_pair(step - FOLD_PAIR_LAG)
        if 0 <= step - FOLD_SIDE_LAG < units:
            fold_side(step - FOLD_SIDE_LAG)

    def sent(step):
        drain(rows.at[:, slot(place)], send_sem.at[step])
        drain(rows.at[:, slot(place)], sum_send_sem.at[step])

    each_step(sent)
    for part in parts:
        side_copy(part).wait_send()
        pair_copy(part).wait_send()
    for part in range(units):
        term_pair(part).wait_send()
        term_side(part).wait_send()
    far_copy.wait_send()
    for copy in (far_keep, far_relay, near_keep, hidden_local, hidden_remote):
        copy.wait()
    drain(sums_out, sum_recv_sem)


def block(tokens, upstream, gate_weight, up_weight, down_weight):
    own_rows, width = tokens.shape
    units = gate_weight.shape[0]
    count = lax.axis_size("blk")
    assert count % 4 == 0 and lax.axis_size("tok") == 2
    line = count // 4
    quarter = line * own_rows
    half = 2 * quarter
    group = 2 * half
    gathers, reduces = len(GATHER_PARTS), len(REDUCE_PARTS)
    bf16, f32 = jnp.bfloat16, jnp.float32
    hbm = pl.BlockSpec(memory_space=pl.ANY)
    dma = pltpu.SemaphoreType.DMA
    return pl.pallas_call(
        block_kernel,
        out_shape=(
            jax.ShapeDtypeStruct((2, 2 * group, width // 2), bf16),
            jax.ShapeDtypeStruct((3, 2 * group, units), bf16),
            jax.ShapeDtypeStruct((2, quarter, width), bf16),
        ),
        in_specs=[hbm] * 5,
        out_specs=(hbm, hbm, hbm),
        scratch_shapes=[
            pltpu.VMEM((3, units, width), bf16),
            pltpu.VMEM((2, group, width), bf16),
            pltpu.VMEM((3, group, units), f32),
            pltpu.VMEM((3, group, units), bf16),
            pltpu.VMEM((2, half, width // 2), bf16),
            pltpu.VMEM((2, half, width), f32),
            pltpu.VMEM((2, half, width), bf16),
            pltpu.VMEM((2, half, width), bf16),
            pltpu.VMEM((2, quarter, width), bf16),
            pltpu.VMEM((2, quarter, width), bf16),
            pltpu.VMEM((2, quarter, width), bf16),
            dma((3, gathers)),
            dma((2,)),
            dma((line,)),
            dma((gathers, line)),
            dma((2, gathers)),
            dma((2, gathers)),
            dma((6,)),
            dma((3,)),
            dma((2, reduces)),
            dma((2, reduces)),
            dma((line,)),
            dma(()),
        ],
        compiler_params=pltpu.CompilerParams(
            collective_id=0, has_side_effects=True, vmem_limit_bytes=VMEM_LIMIT
        ),
    )(tokens, upstream, gate_weight, up_weight, down_weight)


def grad_kernel(
    rows_hbm,
    hidden_hbm,
    sums_hbm,
    mixed,
    input_grad,
    gate_grad,
    up_grad,
    down_grad,
    rows,
    hidden,
    sums,
    tiles,
    load_sems,
    sems,
):
    loads = [
        pltpu.make_async_copy(rows_hbm.at[0], rows.at[0], load_sems.at[0]),
        pltpu.make_async_copy(hidden_hbm.at[0], hidden.at[0], load_sems.at[1]),
        pltpu.make_async_copy(hidden_hbm.at[1], hidden.at[1], load_sems.at[2]),
        pltpu.make_async_copy(rows_hbm.at[1], rows.at[1], load_sems.at[3]),
        pltpu.make_async_copy(hidden_hbm.at[2], hidden.at[2], load_sems.at[4]),
        pltpu.make_async_copy(sums_hbm, sums, load_sems.at[5]),
    ]
    for copy in loads:
        copy.start()
    width = rows.shape[2] // GRAD_CHUNKS
    pending = [None] * GRAD_SLOTS
    step = 0
    for index, result in enumerate((gate_grad, up_grad, down_grad)):
        for copy in (loads[:2], loads[2:3], loads[3:5])[index]:
            copy.wait()
        for part in range(GRAD_CHUNKS):
            cols = pl.ds(part * width, width)
            where = step % GRAD_SLOTS
            if pending[where] is not None:
                pending[where].wait()
            tiles[where] = lax.dot_general(
                hidden[index],
                rows[index // 2, :, cols],
                (((0,), (0,)), ((), ())),
                preferred_element_type=jnp.float32,
            ).astype(jnp.bfloat16)
            pending[where] = pltpu.make_async_copy(
                tiles.at[where], result.at[:, cols], sems.at[where]
            )
            pending[where].start()
            step += 1
    own_rows, quarter = mixed.shape[0], sums.shape[1]
    pick = (
        lax.broadcasted_iota(jnp.int32, (own_rows, quarter), 1) % own_rows
        == lax.broadcasted_iota(jnp.int32, (own_rows, quarter), 0)
    ).astype(jnp.bfloat16)
    loads[5].wait()
    for index, result in enumerate((mixed, input_grad)):
        result[...] = jnp.dot(pick, sums[index], preferred_element_type=jnp.float32).astype(
            jnp.bfloat16
        )
    for copy in pending:
        if copy is not None:
            copy.wait()


def finish(rows, hidden, sums, own_rows):
    units = hidden.shape[2]
    width = rows.shape[2]
    hbm = pl.BlockSpec(memory_space=pl.ANY)
    vmem = pl.BlockSpec(memory_space=pltpu.VMEM)
    small = jax.ShapeDtypeStruct((own_rows, sums.shape[2]), jnp.bfloat16)
    shape = jax.ShapeDtypeStruct((units, width), jnp.bfloat16)
    return pl.pallas_call(
        grad_kernel,
        out_shape=(small, small, shape, shape, shape),
        in_specs=[hbm, hbm, hbm],
        out_specs=(vmem, vmem, hbm, hbm, hbm),
        scratch_shapes=[
            pltpu.VMEM(rows.shape, jnp.bfloat16),
            pltpu.VMEM(hidden.shape, jnp.bfloat16),
            pltpu.VMEM(sums.shape, jnp.bfloat16),
            pltpu.VMEM((GRAD_SLOTS, units, width // GRAD_CHUNKS), jnp.bfloat16),
            pltpu.SemaphoreType.DMA((6,)),
            pltpu.SemaphoreType.DMA((GRAD_SLOTS,)),
        ],
        compiler_params=pltpu.CompilerParams(vmem_limit_bytes=VMEM_LIMIT),
    )(rows, hidden, sums)


def local(tokens, *rest):
    rows, hidden, sums = block(tokens, *rest)
    return finish(rows, hidden, sums, tokens.shape[0])


def solution(mesh):
    return jax.shard_map(
        local,
        mesh=mesh,
        in_specs=(
            P(("blk", "tok"), None),
            P(("blk", "tok"), None),
            P("blk", None),
            P("blk", None),
            P("blk", None),
        ),
        out_specs=(
            P(("blk", "tok"), None),
            P(("blk", "tok"), None),
            P("blk", "tok"),
            P("blk", "tok"),
            P("blk", "tok"),
        ),
        check_vma=False,
    )
```
